32 devices in a mesh: tile: 4 (over y, x), mom: 2 (over core), ewin: 4 (over z).
Axes of the slice: x: 2, y: 2, z: 4, core: 2. Of those that a mesh axis runs over, the one named last changes fastest.
Arguments:
- green_ret: bfloat16 [2, 4, 4, 512, 1024], P('mom', 'ewin', 'tile'), may hold values from -0.25 to 0.25
- injection: float32 [2, 4, 4, 512], P('mom', 'ewin', 'tile'), may hold values from 0.1 to 1
- mom_shift: int32 [4], replicated, may hold values from 0 to 7, as said below
- phon_off: int32 [8], replicated, may hold values from -4 to 4
- coupling: float32 [4, 8], replicated, may hold values from 0.05 to 1
- tile_nbr: int32 [4, 4], replicated, may hold values from 0 to 3
Outputs:
- sigma_less: bfloat16 [2, 4, 4, 512, 1024], P('mom', 'ewin', None, 'tile')
The draws below stay inside these ranges and needn't reach their ends.
Inputs may be any that keep to these rules, and one draw needn't show every extreme that they name: `mom_shift`: every residue from 0 to 1 appears among the 4 shifts taken modulo 2.
All inputs are finite; a program needn't handle non-finite values.
Results may differ from the reference program's by a relative error of at most 0.0036.
Values may be sent and summed in bfloat16 or wider, within the bound.
A program may use at most 64 MiB of HBM per device.

```python
import math
import jax
import jax.numpy as jnp
from jax import lax

ORB = 512
HW = 4
NQ = 4
NW = 8
NB = 4
MOMS = 2
SLABS = 4
TILES = 4
ESLAB = 4


def draw_mom_shift(key, part):
    first_key = jax.random.fold_in(key, 11)
    second_key = jax.random.fold_in(key, 23)
    order_key = jax.random.fold_in(key, 37)
    multi_key = jax.random.fold_in(key, 53)
    residues = jax.random.permutation(first_key, MOMS).astype(jnp.int32)
    multiples = jax.random.randint(multi_key, (MOMS,), 0, 4).astype(jnp.int32)
    multiples = jnp.where(residues == 0, 0, jnp.where(residues == MOMS - 1, 3, multiples)).astype(jnp.int32)
    covered = (residues + MOMS * multiples).astype(jnp.int32)
    extra = jax.random.randint(second_key, (NQ - MOMS,), 0, 4 * MOMS).astype(jnp.int32)
    joined = jnp.concatenate([covered, extra])
    return jax.random.permutation(order_key, joined).astype(jnp.int32)


def place_ends(result, own_key, least, largest):
    place = [jax.random.randint(jax.random.fold_in(own_key, axis), (), 0, length) for axis, length in enumerate(result.shape)]
    longest = result.shape.index(max(result.shape))
    beside = place[:longest] + [(place[longest] + 1) % result.shape[longest]] + place[longest + 1:]
    return result.at[tuple(place)].set(least).at[tuple(beside)].set(largest)


def level_of(key, dims, cuts, smallest, high):
    factor_of, own = 1.0, jax.random.fold_in(key, 6)
    for axis_at, parts in cuts:
        draws = jnp.exp(jax.random.uniform(jax.random.fold_in(own, axis_at), (parts,), jnp.float32, smallest / len(cuts), high / len(cuts)))
        factor_of = factor_of * jnp.repeat(draws, dims[axis_at] // parts).reshape([-1 if axis == axis_at else 1 for axis in range(len(dims))])
    return factor_of


def scatter_about(rng, shape, deviation, reach, split=(), held_as=jnp.bfloat16):
    result = deviation * jax.random.normal(rng, shape, jnp.float32)
    if split:
        result = result * level_of(rng, shape, split, -0.22, 0.18)
    return jnp.clip(result, -reach, reach).astype(held_as)


def setup_inputs(seed: int = 0) -> dict:
    key_of = jax.random.split(jax.random.key(seed), 7)
    return {
        "green_ret": scatter_about(key_of[0], (MOMS, SLABS, ESLAB, ORB, 2 * ORB), ORB ** -0.5, 0.25, ((0, 2), (1, 4), (2, 4))),
        "injection": jnp.clip(jnp.exp(math.log(1.0) - 2.3025851 * jax.random.uniform(key_of[1], (MOMS, SLABS, ESLAB, ORB), jnp.float32) ** level_of(key_of[1], (MOMS, SLABS, ESLAB, ORB), ((0, 2), (1, 4), (2, 4)), -0.2, 0.2)), 0.1, 1.0),
        "mom_shift": draw_mom_shift(jax.random.fold_in(key_of[6], 71), 0),
        "phon_off": place_ends(jax.random.randint(key_of[3], (NW,), 0 - HW, HW + 1), jax.random.fold_in(key_of[3], 1), 0 - HW, HW).astype(jnp.int32),
        "coupling": jnp.clip(jnp.exp(jax.random.uniform(key_of[4], (NQ, NW), jnp.float32, math.log(0.05), math.log(1.0))), 0.05, 1.0),
        "tile_nbr": place_ends(jax.random.randint(key_of[5], (TILES, NB), 0, TILES), jax.random.fold_in(key_of[5], 1), 0, TILES - 1).astype(jnp.int32),
    }


def lesser_point(item):
    block, gamma = item
    re = block[:, :ORB].astype(jnp.float32)
    im = block[:, ORB:].astype(jnp.float32)
    left_re = jnp.concatenate([re * gamma[None, :], im * gamma[None, :]], axis=1).astype(jnp.bfloat16)
    left_im = jnp.concatenate([im * gamma[None, :], -re * gamma[None, :]], axis=1).astype(jnp.bfloat16)
    real = jnp.dot(left_re, block.T, preferred_element_type=jnp.float32)
    imag = jnp.dot(left_im, block.T, preferred_element_type=jnp.float32)
    return jnp.concatenate([real, imag], axis=1).astype(jnp.bfloat16)


def reference(green_ret, injection, mom_shift, phon_off, coupling, tile_nbr):
    moms = green_ret.shape[0]
    energies = green_ret.shape[1] * green_ret.shape[2]
    flat = green_ret.reshape(moms * energies, ORB, 2 * ORB)
    gam = injection.reshape(moms * energies, ORB)
    lesser = lax.map(lesser_point, (flat, gam)).reshape(moms, energies, ORB, 2 * ORB)
    padded = jnp.pad(lesser, ((0, 0), (HW, HW), (0, 0), (0, 0)))
    rows = ORB // TILES
    coltile = jnp.arange(ORB, dtype=jnp.int32) // rows
    colmask = jnp.any(coltile[None, :, None] == tile_nbr[:, None, :], axis=2).astype(jnp.float32)
    full_mask = colmask[coltile]
    full_mask = jnp.concatenate([full_mask, full_mask], axis=1)

    def one_momentum(k):
        acc = jnp.zeros((energies, ORB, 2 * ORB), jnp.float32)
        for s in range(NQ):
            src = jnp.mod(k - mom_shift[s], moms).astype(jnp.int32)
            for o in range(NW):
                start = (HW + phon_off[o]).astype(jnp.int32)
                piece = lax.dynamic_slice(padded, (src, start, jnp.int32(0), jnp.int32(0)), (1, energies, ORB, 2 * ORB))[0]
                acc = acc + coupling[s, o] * piece.astype(jnp.float32)
        return (acc * full_mask[None]).astype(jnp.bfloat16)

    out = lax.map(one_momentum, jnp.arange(moms, dtype=jnp.int32))
    return out.reshape(green_ret.shape)
```

```python
import jax
import jax.numpy as jnp
from jax import lax
from jax.experimental import pallas as pl
from jax.experimental.pallas import tpu as pltpu
from jax.sharding import PartitionSpec as P

HW = 4
NW = 8
PACK = 16
MESH = pl.DeviceIdType.MESH


def fused_kernel(
    nt, nm, nz, g_ref, gam_ref, shift_ref, off_ref, coup_ref, out_ref,
    stage, held, fin, tab, a_send, a_recv, z_send, z_recv, f_send, f_recv, own_sem,
):
    t, m, z = lax.axis_index("tile"), lax.axis_index("mom"), lax.axis_index("ewin")
    groups, steps, rb, width = g_ref.shape
    orb = width // 2
    has_up, has_down = z < nz - 1, z > 0

    def dev(tt, mm, zz):
        return {"tile": tt, "mom": mm, "ewin": zz}

    def tile_at(i):
        return lax.rem(t + i, nt)

    def mom_at(j):
        return lax.rem(m + j, nm)

    pairs = [(i, j) for i in range(nt) for j in range(nm)]
    barrier = pltpu.get_barrier_semaphore()
    for i, j in pairs[1:]:
        pl.semaphore_signal(barrier, inc=1, device_id=dev(tile_at(i), mom_at(j), z), device_id_type=MESH)

    @pl.when(has_up)
    def _():
        pl.semaphore_signal(barrier, inc=1, device_id=dev(t, m, z + 1), device_id_type=MESH)

    @pl.when(has_down)
    def _():
        pl.semaphore_signal(barrier, inc=1, device_id=dev(t, m, z - 1), device_id_type=MESH)

    def lesser(r):
        rows = g_ref[:, r].reshape(groups * rb, width)
        re = rows[:, :orb].astype(jnp.float32) * gam_ref[...]
        im = rows[:, orb:].astype(jnp.float32) * gam_ref[...]
        left_re = jnp.concatenate([re, im], axis=1).astype(jnp.bfloat16)
        left_im = jnp.concatenate([im, -re], axis=1).astype(jnp.bfloat16)
        left = jnp.concatenate([left_re, left_im], axis=0)
        right = g_ref[...].reshape(orb, width)
        both = lax.dot_general(left, right, (((1,), (1,)), ((), ())), preferred_element_type=jnp.float32)
        both = both.astype(jnp.bfloat16)
        half = groups * rb
        stage[r, :, :, :orb] = both[:half].reshape(groups, rb, orb)
        stage[r, :, :, orb:] = both[half:].reshape(groups, rb, orb)

    def source(i):
        return lax.rem(t + nt - i, nt)

    def a_copy(r, i, j):
        return pltpu.make_async_remote_copy(
            src_ref=stage.at[r, tile_at(i) * nm + mom_at(j)],
            dst_ref=held.at[1, t, j, r],
            send_sem=a_send.at[r, i, j],
            recv_sem=a_recv.at[r, i, j],
            device_id=dev(tile_at(i), mom_at(j), z),
            device_id_type=MESH,
        )

    def a_landed(r, i, j):
        p = source(i)
        return pltpu.make_async_remote_copy(
            src_ref=stage.at[r, 0],
            dst_ref=held.at[1, p, j, r],
            send_sem=a_send.at[r, i, j],
            recv_sem=a_recv.at[r, i, j],
            device_id=dev(tile_at(i), mom_at(j), z),
            device_id_type=MESH,
        )

    def own_copy(r):
        return pltpu.make_async_copy(stage.at[r, t * nm + m], held.at[1, t, 0, r], own_sem.at[r])

    def z_copy(r, i, j, up):
        p = source(i)
        return pltpu.make_async_remote_copy(
            src_ref=held.at[1, p, j, r],
            dst_ref=held.at[0 if up else 2, p, j, r],
            send_sem=z_send.at[0 if up else 1, r, i, j],
            recv_sem=z_recv.at[0 if up else 1, r, i, j],
            device_id=dev(t, m, z + 1 if up else z - 1),
            device_id_type=MESH,
        )

    def start_first(r):
        own_copy(r).start()
        for i, j in pairs[1:]:
            a_copy(r, i, j).start()

    lesser(0)
    pl.semaphore_wait(barrier, nt * nm - 1 + has_up.astype(jnp.int32) + has_down.astype(jnp.int32))
    start_first(0)

    @pl.loop(1, steps)
    def _(r):
        lesser(r)
        start_first(r)

    @pl.when(jnp.logical_not(has_down))
    def _():
        held[0] = jnp.zeros(held.shape[1:], held.dtype)

    @pl.when(jnp.logical_not(has_up))
    def _():
        held[2] = jnp.zeros(held.shape[1:], held.dtype)

    def forward(r):
        for i, j in pairs:
            if (i, j) == (0, 0):
                own_copy(r).wait()
            else:
                a_landed(r, i, j).wait_recv()

            @pl.when(has_up)
            def _():
                z_copy(r, i, j, True).start()

            @pl.when(has_down)
            def _():
                z_copy(r, i, j, False).start()

    forward(0)
    if steps > 1:
        forward(1)

    shifts = [lax.rem(lax.rem(shift_ref[s], nm) + nm, nm) for s in range(shift_ref.shape[0])]
    for diff in range(nm):
        per_off = []
        for o in range(NW):
            acc = jnp.float32(0.0)
            for s in range(len(shifts)):
                acc = acc + jnp.where(shifts[s] == diff, coup_ref[s, o], 0.0)
            per_off.append(acc)
        for d in range(2 * HW + 1):
            acc = jnp.float32(0.0)
            for o in range(NW):
                acc = acc + jnp.where(off_ref[o] + HW == d, per_off[o], 0.0)
            tab[diff, d] = acc

    def fin_copy(r, kk):
        return pltpu.make_async_remote_copy(
            src_ref=fin.at[kk - 1, r],
            dst_ref=out_ref.at[:, m, r],
            send_sem=f_send.at[kk - 1, r],
            recv_sem=f_recv.at[kk - 1, r],
            device_id=dev(t, mom_at(kk), z),
            device_id_type=MESH,
        )

    def fin_landed(r, kk):
        return pltpu.make_async_remote_copy(
            src_ref=fin.at[kk - 1, r],
            dst_ref=out_ref.at[:, lax.rem(m + nm - kk, nm), r],
            send_sem=f_send.at[kk - 1, r],
            recv_sem=f_recv.at[kk - 1, r],
            device_id=dev(t, mom_at(kk), z),
            device_id_type=MESH,
        )

    def mix(r):
        for i, j in pairs:
            @pl.when(has_down)
            def _():
                z_copy(r, i, j, True).wait_recv()

            @pl.when(has_up)
            def _():
                z_copy(r, i, j, False).wait_recv()

        weight = [[tab[diff, d] for d in range(2 * HW + 1)] for diff in range(nm)]

        @pl.loop(0, width // 128)
        def _(c):
            cols = pl.ds(pl.multiple_of(c * 128, 128), 128)
            acc = [[None] * nt for _ in range(nm)]
            for zs in range(3):
                for p in range(nt):
                    src = zs * nt + p
                    for j in range(nm):
                        x = held[zs, p, j, r, :, cols].astype(jnp.float32)
                        for kk in range(nm):
                            for e in range(nt):
                                if 0 <= src - e <= 2 * HW:
                                    term = weight[(kk + j) % nm][src - e] * x
                                    acc[kk][e] = term if acc[kk][e] is None else acc[kk][e] + term
            for e in range(nt):
                out_ref[e, m, r, :, cols] = acc[0][e].astype(jnp.bfloat16)
                for kk in range(1, nm):
                    fin[kk - 1, r, e, :, cols] = acc[kk][e].astype(jnp.bfloat16)

        for kk in range(1, nm):
            fin_copy(r, kk).start()

    @pl.loop(0, steps)
    def _(r):
        mix(r)

        @pl.when(r + 2 < steps)
        def _():
            forward(r + 2)

    @pl.loop(0, steps)
    def _(r):
        for kk in range(1, nm):
            fin_copy(r, kk).wait_send()
            fin_landed(r, kk).wait_recv()
        for i, j in pairs:
            if (i, j) != (0, 0):
                a_copy(r, i, j).wait_send()

            @pl.when(has_up)
            def _():
                z_copy(r, i, j, True).wait_send()

            @pl.when(has_down)
            def _():
                z_copy(r, i, j, False).wait_send()


def column_mask(tile_nbr, orbitals, per_tile):
    tile_here = lax.axis_index("tile")
    neighbours = lax.dynamic_index_in_dim(tile_nbr, tile_here, 0, keepdims=False)
    coltile = jnp.arange(orbitals, dtype=jnp.int32) // per_tile
    colmask = jnp.any(coltile[:, None] == neighbours[None, :], axis=1)
    return jnp.concatenate([colmask, colmask])


def fused(green_ret, injection, mom_shift, phon_off, coupling, tile_nbr):
    nt, nm, nz = lax.axis_size("tile"), lax.axis_size("mom"), lax.axis_size("ewin")
    orbitals, width = green_ret.shape[3:]
    per_tile = orbitals // nt
    steps = per_tile // nm // PACK
    green = green_ret.reshape(nt * nm, steps, PACK, width)
    gamma = injection.reshape(1, orbitals)
    vmem, smem = pl.BlockSpec(memory_space=pltpu.VMEM), pl.BlockSpec(memory_space=pltpu.SMEM)
    dma = pltpu.SemaphoreType.DMA
    total = pl.pallas_call(
        lambda *refs: fused_kernel(nt, nm, nz, *refs),
        out_shape=jax.ShapeDtypeStruct((nt, nm, steps, PACK, width), jnp.bfloat16),
        in_specs=[vmem, vmem, smem, smem, smem],
        out_specs=vmem,
        scratch_shapes=[
            pltpu.VMEM((steps, nt * nm, PACK, width), jnp.bfloat16),
            pltpu.VMEM((3, nt, nm, steps, PACK, width), jnp.bfloat16),
            pltpu.VMEM((max(nm - 1, 1), steps, nt, PACK, width), jnp.bfloat16),
            pltpu.SMEM((nm, 2 * HW + 1), jnp.float32),
            dma((steps, nt, nm)),
            dma((steps, nt, nm)),
            dma((2, steps, nt, nm)),
            dma((2, steps, nt, nm)),
            dma((max(nm - 1, 1), steps)),
            dma((max(nm - 1, 1), steps)),
            dma((steps,)),
        ],
        compiler_params=pltpu.CompilerParams(collective_id=0, has_side_effects=True),
    )(green, gamma, mom_shift, phon_off, coupling)
    total = total.reshape(nt, per_tile, width)
    colmask = column_mask(tile_nbr, orbitals, per_tile)
    result = jnp.where(colmask[None, None, :], total, jnp.zeros((), jnp.bfloat16))
    return result[None, None]


def with_halo(shard, sides, width):
    for axis, dim in sides:
        peers, length = (lax.axis_size(axis), shard.shape[dim])
        up = [(i, (i + 1) % peers) for i in range(peers - 1)]
        down = [(j, i) for i, j in up]
        last = lax.slice_in_dim(shard, length - width, length, axis=dim)
        initial = lax.slice_in_dim(shard, 0, width, axis=dim)
        before = lax.ppermute(last, axis, up)
        after = lax.ppermute(initial, axis, down)
        shard = jnp.concatenate([before, shard, after], axis=dim)
    return shard


def on_device(green_ret, injection, mom_shift, phon_off, coupling, tile_nbr):
    blocks = green_ret[0, 0]
    gamma = injection[0, 0]
    orbitals = blocks.shape[1]
    ntiles = lax.axis_size("tile")
    per_tile = orbitals // ntiles
    real_part = blocks[:, :, :orbitals].astype(jnp.float32)
    imag_part = blocks[:, :, orbitals:].astype(jnp.float32)
    scale = gamma[:, None, :]
    left_re = jnp.concatenate([real_part * scale, imag_part * scale], axis=2).astype(jnp.bfloat16)
    left_im = jnp.concatenate([imag_part * scale, -real_part * scale], axis=2).astype(jnp.bfloat16)
    real_out = jnp.einsum("prk,pck->prc", left_re, blocks, preferred_element_type=jnp.float32)
    imag_out = jnp.einsum("prk,pck->prc", left_im, blocks, preferred_element_type=jnp.float32)
    payload = jnp.concatenate([real_out, imag_out], axis=2).astype(jnp.bfloat16)
    exchanged = lax.all_to_all(payload, "tile", split_axis=1, concat_axis=0, tiled=True)
    energies = exchanged.shape[0]
    rimmed = with_halo(exchanged, (("ewin", 0),), HW)
    extended = lax.all_gather(rimmed[None], "mom", axis=0, tiled=True)
    nmom = lax.axis_size("mom")
    here = lax.axis_index("mom")
    source = jnp.mod(here - mom_shift, nmom)
    onehot = (source[:, None] == jnp.arange(nmom, dtype=jnp.int32)[None, :]).astype(jnp.float32)
    weights = jnp.dot(onehot.T, coupling, precision=lax.Precision.HIGHEST)
    total = jnp.zeros(exchanged.shape, jnp.float32)
    for offset in range(NW):
        start = HW + phon_off[offset]
        piece = lax.dynamic_slice_in_dim(extended, start, energies, 1)
        for moment in range(nmom):
            total = total + weights[moment, offset] * piece[moment].astype(jnp.float32)
    tile_here = lax.axis_index("tile")
    neighbours = lax.dynamic_index_in_dim(tile_nbr, tile_here, 0, keepdims=False)
    coltile = jnp.arange(orbitals, dtype=jnp.int32) // per_tile
    colmask = jnp.any(coltile[:, None] == neighbours[None, :], axis=1).astype(jnp.float32)
    colmask = jnp.concatenate([colmask, colmask])
    result = (total * colmask[None, None, :]).astype(jnp.bfloat16)
    return result[None, None]


def body_for(mesh):
    nt, nm = mesh.shape["tile"], mesh.shape["mom"]

    def body(green_ret, *rest):
        points, orbitals = green_ret.shape[2:4]
        aligned = orbitals % (nt * nm * PACK) == 0 and orbitals % 128 == 0
        if aligned and points == 1 and nt == HW:
            return fused(green_ret, *rest)
        return on_device(green_ret, *rest)

    return body


def solution(mesh):
    placed = (
        P("mom", "ewin", "tile", None, None),
        P("mom", "ewin", "tile", None),
        P(),
        P(),
        P(),
        P(),
    )
    return jax.shard_map(
        body_for(mesh),
        mesh=mesh,
        in_specs=placed,
        out_specs=P("mom", "ewin", None, "tile", None),
        check_vma=False,
    )
```

```python
import jax
import jax.numpy as jnp
from jax import lax
from jax.experimental import pallas as pl
from jax.experimental.pallas import tpu as pltpu
from jax.sharding import PartitionSpec as P

HW = 4
NW = 8
LANES = 128
PACK = 16
MESH = pl.DeviceIdType.MESH


def fused_kernel(
    nt, nm, nz, g_ref, gam_ref, shift_ref, off_ref, coup_ref, out_ref,
    left, stage, cross, held, fin, parts, tab,
    a_send, a_recv, z_send, z_recv, f_send, f_recv, own_sem,
):
    t, m, z = lax.axis_index("tile"), lax.axis_index("mom"), lax.axis_index("ewin")
    orb, width = g_ref.shape
    tall = orb // nt
    hr = tall // nm
    qr = hr // 2
    rows_of = ((0, hr), (hr, qr), (hr + qr, hr))
    has_up, has_down = z < nz - 1, z > 0

    def dev(tt, mm, zz):
        return {"tile": tt, "mom": mm, "ewin": zz}

    def order(q):
        return q + (q // 2) * (5 - 2 * q)

    ring = order(t)

    def tile_at(i):
        return order(lax.rem(ring + i, nt))

    def mom_at(j):
        return lax.rem(m + j, nm)

    pairs = [(i, j) for i in range(nt) for j in range(nm)]
    barrier = pltpu.get_barrier_semaphore()
    for i, j in pairs[1:]:
        pl.semaphore_signal(barrier, inc=1, device_id=dev(tile_at(i), mom_at(j), z), device_id_type=MESH)

    @pl.when(has_up)
    def _():
        pl.semaphore_signal(barrier, inc=1, device_id=dev(t, m, z + 1), device_id_type=MESH)

    @pl.when(has_down)
    def _():
        pl.semaphore_signal(barrier, inc=1, device_id=dev(t, m, z - 1), device_id_type=MESH)

    def tile_rows(tile):
        return pl.ds(pl.multiple_of(tile * tall, tall), tall)

    def product(slot, tile):
        both = lax.dot_general(
            left[slot], g_ref[tile_rows(tile), :], (((1,), (1,)), ((), ())), preferred_element_type=jnp.float32
        ).astype(jnp.bfloat16)
        return both[:tall], both[tall:]

    def compute_first(i):
        rows = g_ref[tile_rows(tile_at(i)), :]
        re = rows[:, :orb].astype(jnp.float32) * gam_ref[...]
        im = rows[:, orb:].astype(jnp.float32) * gam_ref[...]
        left[i, :tall, :orb] = re.astype(jnp.bfloat16)
        left[i, :tall, orb:] = im.astype(jnp.bfloat16)
        left[i, tall:, :orb] = im.astype(jnp.bfloat16)
        left[i, tall:, orb:] = (-re).astype(jnp.bfloat16)
        put(0, i, tile_at(i + 1))

    def put(which, i, tile):
        re, im = product(i, tile)
        stage[which, i, :, :, :tall] = re.reshape(nm, hr, tall)
        stage[which, i, :, :, tall:] = im.reshape(nm, hr, tall)

    def compute_cross(a):
        re, im = product(lax.rem(a - ring + nt, nt), order(a + 2))
        cross[a, :, :, :tall] = re.reshape(2 * nm, qr, tall)
        cross[a, :, :, tall:] = im.reshape(2 * nm, qr, tall)

    def unit_source(u, i, j):
        c = mom_at(j)
        if u == 1:
            q = lax.rem(ring + i, nt)
            return cross.at[lax.rem(q, 2), (q // 2) * nm + c]
        return stage.at[u // 2, i, c]

    def a_copy(u, i, j, p):
        lo, n = rows_of[u]
        return pltpu.make_async_remote_copy(
            src_ref=unit_source(u, i, j),
            dst_ref=held.at[1, p, j, pl.ds(lo, n)],
            send_sem=a_send.at[u, i, j],
            recv_sem=a_recv.at[u, i, j],
            device_id=dev(tile_at(i), mom_at(j), z),
            device_id_type=MESH,
        )

    def own_copy(u):
        lo, n = rows_of[u]
        return pltpu.make_async_copy(unit_source(u, 0, 0), held.at[1, t, 0, pl.ds(lo, n)], own_sem.at[u])

    def z_copy(u, i, j, up):
        p = tile_at(nt - i)
        lo, n = rows_of[u]
        return pltpu.make_async_remote_copy(
            src_ref=held.at[1, p, j, pl.ds(lo, n)],
            dst_ref=held.at[0 if up else 2, p, j, pl.ds(lo, n)],
            send_sem=z_send.at[0 if up else 1, u, i, j],
            recv_sem=z_recv.at[0 if up else 1, u, i, j],
            device_id=dev(t, m, z + 1 if up else z - 1),
            device_id_type=MESH,
        )

    def send_slot(u, i):
        for j in range(nm):
            if (i, j) == (0, 0):
                own_copy(u).start()
            else:
                a_copy(u, i, j, t).start()

    def forward(u):
        for i, j in pairs:
            if (i, j) == (0, 0):
                own_copy(u).wait()
            else:
                a_copy(u, i, j, tile_at(nt - i)).wait_recv()

            @pl.when(has_up)
            def _():
                z_copy(u, i, j, True).start()

            @pl.when(has_down)
            def _():
                z_copy(u, i, j, False).start()

    for i in range(nt):
        compute_first(i)
        if i == 0:
            pl.semaphore_wait(barrier, nt * nm - 1 + has_up.astype(jnp.int32) + has_down.astype(jnp.int32))
        send_slot(0, i)
    for a in range(2):
        compute_cross(a)
    for i in range(nt):
        send_slot(1, i)
    forward(0)
    for i in range(nt):
        put(1, i, tile_at(i))
        send_slot(2, i)
    forward(1)

    @pl.when(jnp.logical_not(has_down))
    def _():
        held[0] = jnp.zeros(held.shape[1:], held.dtype)

    @pl.when(jnp.logical_not(has_up))
    def _():
        held[2] = jnp.zeros(held.shape[1:], held.dtype)

    shifts = [lax.rem(lax.rem(shift_ref[s], nm) + nm, nm) for s in range(shift_ref.shape[0])]
    for diff in range(nm):
        per_off = []
        for o in range(NW):
            acc = jnp.float32(0.0)
            for s in range(len(shifts)):
                acc = acc + jnp.where(shifts[s] == diff, coup_ref[s, o], 0.0)
            per_off.append(acc)
        for d in range(2 * HW + 1):
            acc = jnp.float32(0.0)
            for o in range(NW):
                acc = acc + jnp.where(off_ref[o] + HW == d, per_off[o], 0.0)
            tab[diff, d] = acc

    def part_lo(u, who):
        if u == 1:
            return pl.multiple_of(((ring // 2) * nm + who) * qr, qr)
        return pl.multiple_of(who * hr, hr)

    def near_copy(u, kk, who):
        lo, n = rows_of[u]
        return pltpu.make_async_remote_copy(
            src_ref=fin.at[kk, :, pl.ds(lo, n)],
            dst_ref=parts.at[u, :, pl.ds(part_lo(u, who), n)],
            send_sem=f_send.at[0, u, kk],
            recv_sem=f_recv.at[0, u, kk],
            device_id=dev(t, mom_at(kk), z),
            device_id_type=MESH,
        )

    def far_copy(u, kk, lo_there):
        lo, n = rows_of[u]
        return pltpu.make_async_remote_copy(
            src_ref=fin.at[kk, :, pl.ds(lo, n)],
            dst_ref=parts.at[1 if u == 1 else 3, :, pl.ds(lo_there, n)],
            send_sem=f_send.at[1, u, kk],
            recv_sem=f_recv.at[1, u, kk],
            device_id=dev(tile_at(1 + u), mom_at(kk), z),
            device_id_type=MESH,
        )

    def far_lo(u, who):
        if u == 1:
            return pl.multiple_of(((1 - ring // 2) * nm + who) * qr, qr)
        return pl.multiple_of(who * hr, hr)

    def mix(u):
        for i, j in pairs:
            @pl.when(has_down)
            def _():
                z_copy(u, i, j, True).wait_recv()

            @pl.when(has_up)
            def _():
                z_copy(u, i, j, False).wait_recv()

        lo, n = rows_of[u]
        base = part_lo(u, m)
        weight = [[tab[diff, d] for d in range(2 * HW + 1)] for diff in range(nm)]
        wide = 2 * tall // LANES

        @pl.loop(0, n // PACK * wide)
        def _(step):
            r = pl.multiple_of((step // wide) * PACK, PACK)
            rows = pl.ds(pl.multiple_of(lo + r, PACK), PACK)
            cols = pl.ds(pl.multiple_of((step % wide) * LANES, LANES), LANES)
            acc = [[None] * nt for _ in range(nm)]
            for zs in range(3):
                for p in range(nt):
                    src = zs * nt + p
                    for j in range(nm):
                        x = held[zs, p, j, rows, cols].astype(jnp.float32)
                        for kk in range(nm):
                            for e in range(nt):
                                if 0 <= src - e <= 2 * HW:
                                    term = weight[(kk + j) % nm][src - e] * x
                                    acc[kk][e] = term if acc[kk][e] is None else acc[kk][e] + term
            for e in range(nt):
                for kk in range(nm):
                    value = acc[kk][e].astype(jnp.bfloat16)
                    if kk == 0:
                        parts[u, e, pl.ds(pl.multiple_of(base + r, PACK), PACK), cols] = value
                    if kk > 0 or u < 2:
                        fin[kk, e, rows, cols] = value

        for kk in range(nm):
            if u < 2:
                far_copy(u, kk, part_lo(u, m)).start()
            if kk > 0:
                near_copy(u, kk, m).start()

    def landed(u):
        for kk in range(nm):
            who = lax.rem(m + nm - kk, nm)
            if u < 2:
                far_copy(u, kk, far_lo(u, who)).wait_recv()
            if kk > 0:
                near_copy(u, kk, who).wait_recv()

    def store(part, tile, flip):
        @pl.loop(0, nt)
        def _(e):
            re, im = parts[part, e, :, :tall], parts[part, e, :, tall:]
            if flip:
                re = re.astype(jnp.float32).T.astype(jnp.bfloat16)
                im = (-(im.astype(jnp.float32).T)).astype(jnp.bfloat16)
            out_ref[e, :, pl.ds(pl.multiple_of(tile * tall, tall), tall)] = re
            out_ref[e, :, pl.ds(pl.multiple_of(orb + tile * tall, tall), tall)] = im

    mix(0)
    forward(2)
    mix(1)
    landed(0)
    store(0, tile_at(1), False)
    store(3, tile_at(nt - 1), True)
    landed(1)

    @pl.when(ring < 2)
    def _():
        store(1, tile_at(2), False)

    @pl.when(ring >= 2)
    def _():
        store(1, tile_at(2), True)

    mix(2)
    landed(2)
    store(2, t, False)

    for u in range(3):
        for kk in range(nm):
            if u < 2:
                far_copy(u, kk, part_lo(u, m)).wait_send()
            if kk > 0:
                near_copy(u, kk, m).wait_send()
        for i, j in pairs:
            if (i, j) != (0, 0):
                a_copy(u, i, j, t).wait_send()

            @pl.when(has_up)
            def _():
                z_copy(u, i, j, True).wait_send()

            @pl.when(has_down)
            def _():
                z_copy(u, i, j, False).wait_send()


def column_mask(tile_nbr, orbitals, per_tile):
    tile_here = lax.axis_index("tile")
    neighbours = lax.dynamic_index_in_dim(tile_nbr, tile_here, 0, keepdims=False)
    coltile = jnp.arange(orbitals, dtype=jnp.int32) // per_tile
    colmask = jnp.any(coltile[:, None] == neighbours[None, :], axis=1)
    return jnp.concatenate([colmask, colmask])


def fused(green_ret, injection, mom_shift, phon_off, coupling, tile_nbr):
    nt, nm, nz = lax.axis_size("tile"), lax.axis_size("mom"), lax.axis_size("ewin")
    orbitals, width = green_ret.shape[3:]
    tall = orbitals // nt
    hr = tall // nm
    qr = hr // 2
    green = green_ret.reshape(orbitals, width)
    gamma = injection.reshape(1, orbitals)
    vmem, smem = pl.BlockSpec(memory_space=pltpu.VMEM), pl.BlockSpec(memory_space=pltpu.SMEM)
    dma = pltpu.SemaphoreType.DMA
    total = pl.pallas_call(
        lambda *refs: fused_kernel(nt, nm, nz, *refs),
        out_shape=jax.ShapeDtypeStruct((nt, tall, width), jnp.bfloat16),
        in_specs=[vmem, vmem, smem, smem, smem],
        out_specs=vmem,
        scratch_shapes=[
            pltpu.VMEM((nt, 2 * tall, width), jnp.bfloat16),
            pltpu.VMEM((2, nt, nm, hr, 2 * tall), jnp.bfloat16),
            pltpu.VMEM((2, 2 * nm, qr, 2 * tall), jnp.bfloat16),
            pltpu.VMEM((3, nt, nm, 2 * hr + qr, 2 * tall), jnp.bfloat16),
            pltpu.VMEM((nm, nt, 2 * hr + qr, 2 * tall), jnp.bfloat16),
            pltpu.VMEM((4, nt, tall, 2 * tall), jnp.bfloat16),
            pltpu.SMEM((nm, 2 * HW + 1), jnp.float32),
            dma((3, nt, nm)),
            dma((3, nt, nm)),
            dma((2, 3, nt, nm)),
            dma((2, 3, nt, nm)),
            dma((2, 3, nm)),
            dma((2, 3, nm)),
            dma((3,)),
        ],
        compiler_params=pltpu.CompilerParams(collective_id=0, has_side_effects=True),
    )(green, gamma, mom_shift, phon_off, coupling)
    colmask = column_mask(tile_nbr, orbitals, tall)
    result = jnp.where(colmask[None, None, :], total, jnp.zeros((), jnp.bfloat16))
    return result[None, None]


def with_halo(shard, sides, width):
    for axis, dim in sides:
        peers, length = (lax.axis_size(axis), shard.shape[dim])
        up = [(i, (i + 1) % peers) for i in range(peers - 1)]
        down = [(j, i) for i, j in up]
        last = lax.slice_in_dim(shard, length - width, length, axis=dim)
        initial = lax.slice_in_dim(shard, 0, width, axis=dim)
        before = lax.ppermute(last, axis, up)
        after = lax.ppermute(initial, axis, down)
        shard = jnp.concatenate([before, shard, after], axis=dim)
    return shard


def on_device(green_ret, injection, mom_shift, phon_off, coupling, tile_nbr):
    blocks = green_ret[0, 0]
    gamma = injection[0, 0]
    orbitals = blocks.shape[1]
    ntiles = lax.axis_size("tile")
    per_tile = orbitals // ntiles
    real_part = blocks[:, :, :orbitals].astype(jnp.float32)
    imag_part = blocks[:, :, orbitals:].astype(jnp.float32)
    scale = gamma[:, None, :]
    left_re = jnp.concatenate([real_part * scale, imag_part * scale], axis=2).astype(jnp.bfloat16)
    left_im = jnp.concatenate([imag_part * scale, -real_part * scale], axis=2).astype(jnp.bfloat16)
    real_out = jnp.einsum("prk,pck->prc", left_re, blocks, preferred_element_type=jnp.float32)
    imag_out = jnp.einsum("prk,pck->prc", left_im, blocks, preferred_element_type=jnp.float32)
    payload = jnp.concatenate([real_out, imag_out], axis=2).astype(jnp.bfloat16)
    exchanged = lax.all_to_all(payload, "tile", split_axis=1, concat_axis=0, tiled=True)
    energies = exchanged.shape[0]
    rimmed = with_halo(exchanged, (("ewin", 0),), HW)
    extended = lax.all_gather(rimmed[None], "mom", axis=0, tiled=True)
    nmom = lax.axis_size("mom")
    here = lax.axis_index("mom")
    source = jnp.mod(here - mom_shift, nmom)
    onehot = (source[:, None] == jnp.arange(nmom, dtype=jnp.int32)[None, :]).astype(jnp.float32)
    weights = jnp.dot(onehot.T, coupling, precision=lax.Precision.HIGHEST)
    total = jnp.zeros(exchanged.shape, jnp.float32)
    for offset in range(NW):
        start = HW + phon_off[offset]
        piece = lax.dynamic_slice_in_dim(extended, start, energies, 1)
        for moment in range(nmom):
            total = total + weights[moment, offset] * piece[moment].astype(jnp.float32)
    tile_here = lax.axis_index("tile")
    neighbours = lax.dynamic_index_in_dim(tile_nbr, tile_here, 0, keepdims=False)
    coltile = jnp.arange(orbitals, dtype=jnp.int32) // per_tile
    colmask = jnp.any(coltile[:, None] == neighbours[None, :], axis=1).astype(jnp.float32)
    colmask = jnp.concatenate([colmask, colmask])
    result = (total * colmask[None, None, :]).astype(jnp.bfloat16)
    return result[None, None]


def body_for(mesh):
    nt, nm = mesh.shape["tile"], mesh.shape["mom"]

    def body(green_ret, *rest):
        points, orbitals = green_ret.shape[2:4]
        aligned = orbitals % (nt * LANES) == 0 and orbitals % (nt * nm * 2 * PACK) == 0
        if aligned and points == 1 and nt == HW:
            return fused(green_ret, *rest)
        return on_device(green_ret, *rest)

    return body


def solution(mesh):
    placed = (
        P("mom", "ewin", "tile", None, None),
        P("mom", "ewin", "tile", None),
        P(),
        P(),
        P(),
        P(),
    )
    return jax.shard_map(
        body_for(mesh),
        mesh=mesh,
        in_specs=placed,
        out_specs=P("mom", "ewin", None, "tile", None),
        check_vma=False,
    )
```

```python
import jax
import jax.numpy as jnp
from jax import lax
from jax.experimental import pallas as pl
from jax.experimental.pallas import tpu as pltpu
from jax.sharding import PartitionSpec as P

HW = 4
NW = 8
LANES = 128
PACK = 16
MESH = pl.DeviceIdType.MESH


def fused_kernel(
    nt, nm, nz, g_ref, gam_ref, shift_ref, off_ref, coup_ref, out_ref,
    left, stage, cross, diag, held, fin, parts, tab,
    a_send, a_recv, z_send, z_recv, f_send, f_recv, own_sem,
):
    t, m, z = lax.axis_index("tile"), lax.axis_index("mom"), lax.axis_index("ewin")
    orb, width = g_ref.shape
    tall = orb // nt
    qr = tall // nm // 2
    has_up, has_down = z < nz - 1, z > 0

    def dev(tt, mm, zz):
        return {"tile": tt, "mom": mm, "ewin": zz}

    def order(q):
        return q + (q // 2) * (5 - 2 * q)

    ring = order(t)

    def tile_at(i):
        return order(lax.rem(ring + i, nt))

    def mom_at(j):
        return lax.rem(m + j, nm)

    pairs = [(i, j) for i in range(nt) for j in range(nm)]
    barrier = pltpu.get_barrier_semaphore()
    for i, j in pairs[1:]:
        pl.semaphore_signal(barrier, inc=1, device_id=dev(tile_at(i), mom_at(j), z), device_id_type=MESH)

    @pl.when(has_up)
    def _():
        pl.semaphore_signal(barrier, inc=1, device_id=dev(t, m, z + 1), device_id_type=MESH)

    @pl.when(has_down)
    def _():
        pl.semaphore_signal(barrier, inc=1, device_id=dev(t, m, z - 1), device_id_type=MESH)

    def tile_rows(tile):
        return pl.ds(pl.multiple_of(tile * tall, tall), tall)

    def product(slot, tile):
        both = lax.dot_general(
            left[slot], g_ref[tile_rows(tile), :], (((1,), (1,)), ((), ())), preferred_element_type=jnp.float32
        )
        return both[:tall], both[tall:]

    def compute_first(i):
        rows = g_ref[tile_rows(tile_at(i)), :]
        re = rows[:, :orb].astype(jnp.float32) * gam_ref[...]
        im = rows[:, orb:].astype(jnp.float32) * gam_ref[...]
        left[i, :tall, :orb] = re.astype(jnp.bfloat16)
        left[i, :tall, orb:] = im.astype(jnp.bfloat16)
        left[i, tall:, :orb] = im.astype(jnp.bfloat16)
        left[i, tall:, orb:] = (-re).astype(jnp.bfloat16)
        put(i, tile_at(i + 1))

    def triangle():
        return (lax.broadcasted_iota(jnp.int32, (tall, tall), d) for d in (0, 1))

    def put(i, tile):
        re, im = product(i, tile)
        stage[i, :, :, :, :tall] = re.reshape(2, nm, qr, tall).astype(jnp.bfloat16)
        stage[i, :, :, :, tall:] = im.reshape(2, nm, qr, tall).astype(jnp.bfloat16)

    def put_diagonal(i):
        re, im = product(i, tile_at(i))
        row, col = triangle()
        both = jnp.where(row > col, im, re).reshape(nm, 2, qr, tall).astype(jnp.bfloat16)
        diag[i, :, :, :tall] = both[:, 0]
        diag[i, :, :, tall:] = both[:, 1]

    def compute_cross(a):
        re, im = product(lax.rem(a - ring + nt, nt), order(a + 2))
        cross[a, :, :, :tall] = re.reshape(2 * nm, qr, tall).astype(jnp.bfloat16)
        cross[a, :, :, tall:] = im.reshape(2 * nm, qr, tall).astype(jnp.bfloat16)

    def unit_source(u, i, j):
        c = mom_at(j)
        if u == 0:
            return stage.at[i, 0, c]
        if u == 1:
            return stage.at[(i - 1) % nt, 1, c]
        if u == 2:
            q = lax.rem(ring + i, nt)
            return cross.at[lax.rem(q, 2), (q // 2) * nm + c]
        return diag.at[i, c]

    def a_copy(u, i, j, p):
        lo, n = u * qr, qr
        return pltpu.make_async_remote_copy(
            src_ref=unit_source(u, i, j),
            dst_ref=held.at[1, p, j, pl.ds(lo, n)],
            send_sem=a_send.at[u, i, j],
            recv_sem=a_recv.at[u, i, j],
            device_id=dev(tile_at(i), mom_at(j), z),
            device_id_type=MESH,
        )

    def own_copy(u):
        lo, n = u * qr, qr
        return pltpu.make_async_copy(unit_source(u, 0, 0), held.at[1, t, 0, pl.ds(lo, n)], own_sem.at[u])

    def z_copy(u, i, j, up):
        p = tile_at(nt - i)
        lo, n = u * qr, qr
        return pltpu.make_async_remote_copy(
            src_ref=held.at[1, p, j, pl.ds(lo, n)],
            dst_ref=held.at[0 if up else 2, p, j, pl.ds(lo, n)],
            send_sem=z_send.at[0 if up else 1, u, i, j],
            recv_sem=z_recv.at[0 if up else 1, u, i, j],
            device_id=dev(t, m, z + 1 if up else z - 1),
            device_id_type=MESH,
        )

    def send_slot(u, i):
        for j in range(nm):
            if (i, j) == (0, 0):
                own_copy(u).start()
            else:
                a_copy(u, i, j, t).start()

    def forward(u):
        for i, j in pairs:
            if (i, j) == (0, 0):
                own_copy(u).wait()
            else:
                a_copy(u, i, j, tile_at(nt - i)).wait_recv()

            @pl.when(has_up)
            def _():
                z_copy(u, i, j, True).start()

            @pl.when(has_down)
            def _():
                z_copy(u, i, j, False).start()

    for i in range(nt):
        compute_first(i)
        if i == 0:
            pl.semaphore_wait(barrier, nt * nm - 1 + has_up.astype(jnp.int32) + has_down.astype(jnp.int32))
        send_slot(0, i)
    for i in range(nt):
        send_slot(1, i)
    for a in range(2):
        compute_cross(a)
    for i in range(nt):
        send_slot(2, i)
    forward(0)
    for i in range(nt):
        put_diagonal(i)
        send_slot(3, i)
    forward(1)

    @pl.when(jnp.logical_not(has_down))
    def _():
        held[0] = jnp.zeros(held.shape[1:], held.dtype)

    @pl.when(jnp.logical_not(has_up))
    def _():
        held[2] = jnp.zeros(held.shape[1:], held.dtype)

    shifts = [lax.rem(lax.rem(shift_ref[s], nm) + nm, nm) for s in range(shift_ref.shape[0])]
    for diff in range(nm):
        per_off = []
        for o in range(NW):
            acc = jnp.float32(0.0)
            for s in range(len(shifts)):
                acc = acc + jnp.where(shifts[s] == diff, coup_ref[s, o], 0.0)
            per_off.append(acc)
        for d in range(2 * HW + 1):
            acc = jnp.float32(0.0)
            for o in range(NW):
                acc = acc + jnp.where(off_ref[o] + HW == d, per_off[o], 0.0)
            tab[diff, d] = acc

    def part_lo(u, who, mine=True):
        block = (0, 1, ring // 2 if mine else 1 - ring // 2, 0)[u]
        return pl.multiple_of((block * nm + who) * qr, qr)

    def near_copy(u, kk, who):
        lo, n = u * qr, qr
        return pltpu.make_async_remote_copy(
            src_ref=fin.at[kk, :, pl.ds(lo, n)],
            dst_ref=parts.at[u, :, pl.ds(part_lo(u, who), n)],
            send_sem=f_send.at[0, u, kk],
            recv_sem=f_recv.at[0, u, kk],
            device_id=dev(t, mom_at(kk), z),
            device_id_type=MESH,
        )

    def far_copy(u, kk, lo_there):
        lo, n = u * qr, qr
        return pltpu.make_async_remote_copy(
            src_ref=fin.at[kk, :, pl.ds(lo, n)],
            dst_ref=parts.at[(1, 0, 2)[u], :, pl.ds(lo_there, n)],
            send_sem=f_send.at[1, u, kk],
            recv_sem=f_recv.at[1, u, kk],
            device_id=dev(tile_at((1, nt - 1, 2)[u]), mom_at(kk), z),
            device_id_type=MESH,
        )

    def mix(u):
        for i, j in pairs:
            @pl.when(has_down)
            def _():
                z_copy(u, i, j, True).wait_recv()

            @pl.when(has_up)
            def _():
                z_copy(u, i, j, False).wait_recv()

        lo, n = u * qr, qr
        base = part_lo(u, m)
        weight = [[tab[diff, d] for d in range(2 * HW + 1)] for diff in range(nm)]
        wide = 2 * tall // LANES

        @pl.loop(0, n // PACK * wide)
        def _(step):
            r = pl.multiple_of((step // wide) * PACK, PACK)
            rows = pl.ds(pl.multiple_of(lo + r, PACK), PACK)
            cols = pl.ds(pl.multiple_of((step % wide) * LANES, LANES), LANES)
            acc = [[None] * nt for _ in range(nm)]
            for zs in range(3):
                for p in range(nt):
                    src = zs * nt + p
                    for j in range(nm):
                        x = held[zs, p, j, rows, cols].astype(jnp.float32)
                        for kk in range(nm):
                            for e in range(nt):
                                if 0 <= src - e <= 2 * HW:
                                    term = weight[(kk + j) % nm][src - e] * x
                                    acc[kk][e] = term if acc[kk][e] is None else acc[kk][e] + term
            for e in range(nt):
                for kk in range(nm):
                    value = acc[kk][e].astype(jnp.bfloat16)
                    if kk == 0:
                        parts[u, e, pl.ds(pl.multiple_of(base + r, PACK), PACK), cols] = value
                    if kk > 0 or u < 3:
                        fin[kk, e, rows, cols] = value

        for kk in range(nm):
            if u < 3:
                far_copy(u, kk, part_lo(u, m)).start()
            if kk > 0:
                near_copy(u, kk, m).start()

    def landed(u):
        for kk in range(nm):
            who = lax.rem(m + nm - kk, nm)
            if u < 3:
                far_copy(u, kk, part_lo(u, who, False)).wait_recv()
            if kk > 0:
                near_copy(u, kk, who).wait_recv()

    def store(part, tile, flip):
        @pl.loop(0, nt)
        def _(e):
            re, im = parts[part, e, :, :tall], parts[part, e, :, tall:]
            if flip:
                re = re.astype(jnp.float32).T.astype(jnp.bfloat16)
                im = (-(im.astype(jnp.float32).T)).astype(jnp.bfloat16)
            out_ref[e, :, pl.ds(pl.multiple_of(tile * tall, tall), tall)] = re
            out_ref[e, :, pl.ds(pl.multiple_of(orb + tile * tall, tall), tall)] = im

    def store_diagonal():
        row, col = triangle()

        @pl.loop(0, nt)
        def _(e):
            packed = [
                parts[3, e, c * qr : (c + 1) * qr, h * tall : (h + 1) * tall] for c in range(nm) for h in range(2)
            ]
            both = jnp.concatenate(packed, axis=0).astype(jnp.float32)
            turned = both.T
            re = jnp.where(row > col, turned, both)
            im = jnp.where(row > col, both, jnp.where(row < col, -turned, 0.0))
            out_ref[e, :, pl.ds(pl.multiple_of(t * tall, tall), tall)] = re.astype(jnp.bfloat16)
            out_ref[e, :, pl.ds(pl.multiple_of(orb + t * tall, tall), tall)] = im.astype(jnp.bfloat16)

    forward(2)
    mix(0)
    forward(3)
    mix(1)
    mix(2)
    landed(0)
    landed(1)
    store(0, tile_at(1), False)
    store(1, tile_at(nt - 1), True)
    mix(3)
    landed(2)

    @pl.when(ring < 2)
    def _():
        store(2, tile_at(2), False)

    @pl.when(ring >= 2)
    def _():
        store(2, tile_at(2), True)

    landed(3)
    store_diagonal()

    for u in range(4):
        for kk in range(nm):
            if u < 3:
                far_copy(u, kk, part_lo(u, m)).wait_send()
            if kk > 0:
                near_copy(u, kk, m).wait_send()
        for i, j in pairs:
            if (i, j) != (0, 0):
                a_copy(u, i, j, t).wait_send()

            @pl.when(has_up)
            def _():
                z_copy(u, i, j, True).wait_send()

            @pl.when(has_down)
            def _():
                z_copy(u, i, j, False).wait_send()


def column_mask(tile_nbr, orbitals, per_tile):
    tile_here = lax.axis_index("tile")
    neighbours = lax.dynamic_index_in_dim(tile_nbr, tile_here, 0, keepdims=False)
    coltile = jnp.arange(orbitals, dtype=jnp.int32) // per_tile
    colmask = jnp.any(coltile[:, None] == neighbours[None, :], axis=1)
    return jnp.concatenate([colmask, colmask])


def fused(green_ret, injection, mom_shift, phon_off, coupling, tile_nbr):
    nt, nm, nz = lax.axis_size("tile"), lax.axis_size("mom"), lax.axis_size("ewin")
    orbitals, width = green_ret.shape[3:]
    tall = orbitals // nt
    qr = tall // nm // 2
    green = green_ret.reshape(orbitals, width)
    gamma = injection.reshape(1, orbitals)
    vmem, smem = pl.BlockSpec(memory_space=pltpu.VMEM), pl.BlockSpec(memory_space=pltpu.SMEM)
    dma = pltpu.SemaphoreType.DMA
    total = pl.pallas_call(
        lambda *refs: fused_kernel(nt, nm, nz, *refs),
        out_shape=jax.ShapeDtypeStruct((nt, tall, width), jnp.bfloat16),
        in_specs=[vmem, vmem, smem, smem, smem],
        out_specs=vmem,
        scratch_shapes=[
            pltpu.VMEM((nt, 2 * tall, width), jnp.bfloat16),
            pltpu.VMEM((nt, 2, nm, qr, 2 * tall), jnp.bfloat16),
            pltpu.VMEM((2, 2 * nm, qr, 2 * tall), jnp.bfloat16),
            pltpu.VMEM((nt, nm, qr, 2 * tall), jnp.bfloat16),
            pltpu.VMEM((3, nt, nm, 4 * qr, 2 * tall), jnp.bfloat16),
            pltpu.VMEM((nm, nt, 4 * qr, 2 * tall), jnp.bfloat16),
            pltpu.VMEM((4, nt, tall, 2 * tall), jnp.bfloat16),
            pltpu.SMEM((nm, 2 * HW + 1), jnp.float32),
            dma((4, nt, nm)),
            dma((4, nt, nm)),
            dma((2, 4, nt, nm)),
            dma((2, 4, nt, nm)),
            dma((2, 4, nm)),
            dma((2, 4, nm)),
            dma((4,)),
        ],
        compiler_params=pltpu.CompilerParams(collective_id=0, has_side_effects=True),
    )(green, gamma, mom_shift, phon_off, coupling)
    colmask = column_mask(tile_nbr, orbitals, tall)
    result = jnp.where(colmask[None, None, :], total, jnp.zeros((), jnp.bfloat16))
    return result[None, None]


def with_halo(shard, sides, width):
    for axis, dim in sides:
        peers, length = (lax.axis_size(axis), shard.shape[dim])
        up = [(i, (i + 1) % peers) for i in range(peers - 1)]
        down = [(j, i) for i, j in up]
        last = lax.slice_in_dim(shard, length - width, length, axis=dim)
        initial = lax.slice_in_dim(shard, 0, width, axis=dim)
        before = lax.ppermute(last, axis, up)
        after = lax.ppermute(initial, axis, down)
        shard = jnp.concatenate([before, shard, after], axis=dim)
    return shard


def on_device(green_ret, injection, mom_shift, phon_off, coupling, tile_nbr):
    blocks = green_ret[0, 0]
    gamma = injection[0, 0]
    orbitals = blocks.shape[1]
    ntiles = lax.axis_size("tile")
    per_tile = orbitals // ntiles
    real_part = blocks[:, :, :orbitals].astype(jnp.float32)
    imag_part = blocks[:, :, orbitals:].astype(jnp.float32)
    scale = gamma[:, None, :]
    left_re = jnp.concatenate([real_part * scale, imag_part * scale], axis=2).astype(jnp.bfloat16)
    left_im = jnp.concatenate([imag_part * scale, -real_part * scale], axis=2).astype(jnp.bfloat16)
    real_out = jnp.einsum("prk,pck->prc", left_re, blocks, preferred_element_type=jnp.float32)
    imag_out = jnp.einsum("prk,pck->prc", left_im, blocks, preferred_element_type=jnp.float32)
    payload = jnp.concatenate([real_out, imag_out], axis=2).astype(jnp.bfloat16)
    exchanged = lax.all_to_all(payload, "tile", split_axis=1, concat_axis=0, tiled=True)
    energies = exchanged.shape[0]
    rimmed = with_halo(exchanged, (("ewin", 0),), HW)
    extended = lax.all_gather(rimmed[None], "mom", axis=0, tiled=True)
    nmom = lax.axis_size("mom")
    here = lax.axis_index("mom")
    source = jnp.mod(here - mom_shift, nmom)
    onehot = (source[:, None] == jnp.arange(nmom, dtype=jnp.int32)[None, :]).astype(jnp.float32)
    weights = jnp.dot(onehot.T, coupling, precision=lax.Precision.HIGHEST)
    total = jnp.zeros(exchanged.shape, jnp.float32)
    for offset in range(NW):
        start = HW + phon_off[offset]
        piece = lax.dynamic_slice_in_dim(extended, start, energies, 1)
        for moment in range(nmom):
            total = total + weights[moment, offset] * piece[moment].astype(jnp.float32)
    tile_here = lax.axis_index("tile")
    neighbours = lax.dynamic_index_in_dim(tile_nbr, tile_here, 0, keepdims=False)
    coltile = jnp.arange(orbitals, dtype=jnp.int32) // per_tile
    colmask = jnp.any(coltile[:, None] == neighbours[None, :], axis=1).astype(jnp.float32)
    colmask = jnp.concatenate([colmask, colmask])
    result = (total * colmask[None, None, :]).astype(jnp.bfloat16)
    return result[None, None]


def body_for(mesh):
    nt, nm = mesh.shape["tile"], mesh.shape["mom"]

    def body(green_ret, *rest):
        points, orbitals = green_ret.shape[2:4]
        aligned = orbitals % (nt * LANES) == 0 and orbitals % (nt * nm * 2 * PACK) == 0
        if aligned and points == 1 and nt == HW:
            return fused(green_ret, *rest)
        return on_device(green_ret, *rest)

    return body


def solution(mesh):
    placed = (
        P("mom", "ewin", "tile", None, None),
        P("mom", "ewin", "tile", None),
        P(),
        P(),
        P(),
        P(),
    )
    return jax.shard_map(
        body_for(mesh),
        mesh=mesh,
        in_specs=placed,
        out_specs=P("mom", "ewin", None, "tile", None),
        check_vma=False,
    )
```

```python
import jax
import jax.numpy as jnp
from jax import lax
from jax.experimental import pallas as pl
from jax.experimental.pallas import tpu as pltpu
from jax.sharding import PartitionSpec as P

HW = 4
NW = 8
LANES = 128
PACK = 16
MESH = pl.DeviceIdType.MESH


def fused_kernel(
    nt, nm, nz, g_ref, gam_ref, shift_ref, off_ref, coup_ref, nbr_ref, out_ref,
    left, stage, cross, diag, held, fin, parts, tab,
    a_send, a_recv, z_send, z_recv, f_send, f_recv, own_sem,
):
    t, m, z = lax.axis_index("tile"), lax.axis_index("mom"), lax.axis_index("ewin")
    orb, width = g_ref.shape
    tall = orb // nt
    qr = tall // nm // 2
    has_up, has_down = z < nz - 1, z > 0

    def dev(tt, mm, zz):
        return {"tile": tt, "mom": mm, "ewin": zz}

    def order(q):
        return q + (q // 2) * (5 - 2 * q)

    ring = order(t)

    def tile_at(i):
        return order(lax.rem(ring + i, nt))

    def mom_at(j):
        return lax.rem(m + j, nm)

    pairs = [(i, j) for i in range(nt) for j in range(nm)]
    barrier = pltpu.get_barrier_semaphore()
    for i, j in pairs[1:]:
        pl.semaphore_signal(barrier, inc=1, device_id=dev(tile_at(i), mom_at(j), z), device_id_type=MESH)

    @pl.when(has_up)
    def _():
        pl.semaphore_signal(barrier, inc=1, device_id=dev(t, m, z + 1), device_id_type=MESH)

    @pl.when(has_down)
    def _():
        pl.semaphore_signal(barrier, inc=1, device_id=dev(t, m, z - 1), device_id_type=MESH)

    def tile_rows(tile):
        return pl.ds(pl.multiple_of(tile * tall, tall), tall)

    def product(slot, tile):
        both = lax.dot_general(
            left[slot], g_ref[tile_rows(tile), :], (((1,), (1,)), ((), ())), preferred_element_type=jnp.float32
        )
        return both[:tall], both[tall:]

    def compute_first(i):
        rows = g_ref[tile_rows(tile_at(i)), :]
        re = rows[:, :orb].astype(jnp.float32) * gam_ref[...]
        im = rows[:, orb:].astype(jnp.float32) * gam_ref[...]
        left[i, :tall, :orb] = re.astype(jnp.bfloat16)
        left[i, :tall, orb:] = im.astype(jnp.bfloat16)
        left[i, tall:, :orb] = im.astype(jnp.bfloat16)
        left[i, tall:, orb:] = (-re).astype(jnp.bfloat16)
        put(i, tile_at(i + 1))

    def triangle():
        return (lax.broadcasted_iota(jnp.int32, (tall, tall), d) for d in (0, 1))

    def put(i, tile):
        re, im = product(i, tile)
        stage[i, :, :, :, :tall] = re.reshape(2, nm, qr, tall).astype(jnp.bfloat16)
        stage[i, :, :, :, tall:] = im.reshape(2, nm, qr, tall).astype(jnp.bfloat16)

    def put_diagonal(i):
        re, im = product(i, tile_at(i))
        row, col = triangle()
        both = jnp.where(row > col, im, re).reshape(nm, 2, qr, tall).astype(jnp.bfloat16)
        diag[i, :, :, :tall] = both[:, 0]
        diag[i, :, :, tall:] = both[:, 1]

    def compute_cross(a):
        re, im = product(lax.rem(a - ring + nt, nt), order(a + 2))
        cross[a, :, :, :tall] = re.reshape(2 * nm, qr, tall).astype(jnp.bfloat16)
        cross[a, :, :, tall:] = im.reshape(2 * nm, qr, tall).astype(jnp.bfloat16)

    def unit_source(u, i, j):
        c = mom_at(j)
        if u == 0:
            return stage.at[i, 0, c]
        if u == 1:
            return stage.at[(i - 1) % nt, 1, c]
        if u == 2:
            q = lax.rem(ring + i, nt)
            return cross.at[lax.rem(q, 2), (q // 2) * nm + c]
        return diag.at[i, c]

    def a_copy(u, i, j, p):
        lo, n = u * qr, qr
        return pltpu.make_async_remote_copy(
            src_ref=unit_source(u, i, j),
            dst_ref=held.at[1, p, j, pl.ds(lo, n)],
            send_sem=a_send.at[u, i, j],
            recv_sem=a_recv.at[u, i, j],
            device_id=dev(tile_at(i), mom_at(j), z),
            device_id_type=MESH,
        )

    def own_copy(u):
        lo, n = u * qr, qr
        return pltpu.make_async_copy(unit_source(u, 0, 0), held.at[1, t, 0, pl.ds(lo, n)], own_sem.at[u])

    def z_copy(u, i, j, up):
        p = tile_at(nt - i)
        lo, n = u * qr, qr
        return pltpu.make_async_remote_copy(
            src_ref=held.at[1, p, j, pl.ds(lo, n)],
            dst_ref=held.at[0 if up else 2, p, j, pl.ds(lo, n)],
            send_sem=z_send.at[0 if up else 1, u, i, j],
            recv_sem=z_recv.at[0 if up else 1, u, i, j],
            device_id=dev(t, m, z + 1 if up else z - 1),
            device_id_type=MESH,
        )

    def send_slot(u, i):
        for j in range(nm):
            if (i, j) == (0, 0):
                own_copy(u).start()
            else:
                a_copy(u, i, j, t).start()

    def forward(u):
        for i, j in pairs:
            if (i, j) == (0, 0):
                own_copy(u).wait()
            else:
                a_copy(u, i, j, tile_at(nt - i)).wait_recv()

            @pl.when(has_up)
            def _():
                z_copy(u, i, j, True).start()

            @pl.when(has_down)
            def _():
                z_copy(u, i, j, False).start()

    for i in range(nt):
        compute_first(i)
        if i == 0:
            pl.semaphore_wait(barrier, nt * nm - 1 + has_up.astype(jnp.int32) + has_down.astype(jnp.int32))
        send_slot(0, i)
    for i in range(nt):
        send_slot(1, i)
    for a in range(2):
        compute_cross(a)
    for i in range(nt):
        send_slot(2, i)
    forward(0)
    for i in range(nt):
        put_diagonal(i)
        send_slot(3, i)
    forward(1)

    @pl.when(jnp.logical_not(has_down))
    def _():
        held[0] = jnp.zeros(held.shape[1:], held.dtype)

    @pl.when(jnp.logical_not(has_up))
    def _():
        held[2] = jnp.zeros(held.shape[1:], held.dtype)

    shifts = [lax.rem(lax.rem(shift_ref[s], nm) + nm, nm) for s in range(shift_ref.shape[0])]
    for diff in range(nm):
        per_off = []
        for o in range(NW):
            acc = jnp.float32(0.0)
            for s in range(len(shifts)):
                acc = acc + jnp.where(shifts[s] == diff, coup_ref[s, o], 0.0)
            per_off.append(acc)
        for d in range(2 * HW + 1):
            acc = jnp.float32(0.0)
            for o in range(NW):
                acc = acc + jnp.where(off_ref[o] + HW == d, per_off[o], 0.0)
            tab[diff, d] = acc

    def part_lo(u, who, mine=True):
        block = (0, 1, ring // 2 if mine else 1 - ring // 2, 0)[u]
        return pl.multiple_of((block * nm + who) * qr, qr)

    def near_copy(u, kk, who):
        lo, n = u * qr, qr
        return pltpu.make_async_remote_copy(
            src_ref=fin.at[kk, :, pl.ds(lo, n)],
            dst_ref=parts.at[u, :, pl.ds(part_lo(u, who), n)],
            send_sem=f_send.at[0, u, kk],
            recv_sem=f_recv.at[0, u, kk],
            device_id=dev(t, mom_at(kk), z),
            device_id_type=MESH,
        )

    def far_copy(u, kk, lo_there):
        lo, n = u * qr, qr
        return pltpu.make_async_remote_copy(
            src_ref=fin.at[kk, :, pl.ds(lo, n)],
            dst_ref=parts.at[(1, 0, 2)[u], :, pl.ds(lo_there, n)],
            send_sem=f_send.at[1, u, kk],
            recv_sem=f_recv.at[1, u, kk],
            device_id=dev(tile_at((1, nt - 1, 2)[u]), mom_at(kk), z),
            device_id_type=MESH,
        )

    def mix(u):
        for i, j in pairs:
            @pl.when(has_down)
            def _():
                z_copy(u, i, j, True).wait_recv()

            @pl.when(has_up)
            def _():
                z_copy(u, i, j, False).wait_recv()

        lo, n = u * qr, qr
        base = part_lo(u, m)
        weight = [[tab[diff, d] for d in range(2 * HW + 1)] for diff in range(nm)]
        wide = 2 * tall // LANES

        @pl.loop(0, n // PACK * wide)
        def _(step):
            r = pl.multiple_of((step // wide) * PACK, PACK)
            rows = pl.ds(pl.multiple_of(lo + r, PACK), PACK)
            cols = pl.ds(pl.multiple_of((step % wide) * LANES, LANES), LANES)
            acc = [[None] * nt for _ in range(nm)]
            for zs in range(3):
                for p in range(nt):
                    src = zs * nt + p
                    for j in range(nm):
                        x = held[zs, p, j, rows, cols].astype(jnp.float32)
                        for kk in range(nm):
                            for e in range(nt):
                                if 0 <= src - e <= 2 * HW:
                                    term = weight[(kk + j) % nm][src - e] * x
                                    acc[kk][e] = term if acc[kk][e] is None else acc[kk][e] + term
            for e in range(nt):
                for kk in range(nm):
                    value = acc[kk][e].astype(jnp.bfloat16)
                    if kk == 0:
                        parts[u, e, pl.ds(pl.multiple_of(base + r, PACK), PACK), cols] = value
                    if kk > 0 or u < 3:
                        fin[kk, e, rows, cols] = value

        for kk in range(nm):
            if u < 3:
                far_copy(u, kk, part_lo(u, m)).start()
            if kk > 0:
                near_copy(u, kk, m).start()

    def landed(u):
        for kk in range(nm):
            who = lax.rem(m + nm - kk, nm)
            if u < 3:
                far_copy(u, kk, part_lo(u, who, False)).wait_recv()
            if kk > 0:
                near_copy(u, kk, who).wait_recv()

    def kept(tile):
        found = jnp.float32(0.0)
        for b in range(nbr_ref.shape[1]):
            found = jnp.where(nbr_ref[t, b] == tile, 1.0, found)
        return found

    def store(part, tile, flip):
        keep = kept(tile)

        @pl.loop(0, nt)
        def _(e):
            re, im = parts[part, e, :, :tall].astype(jnp.float32), parts[part, e, :, tall:].astype(jnp.float32)
            if flip:
                re, im = re.T, -im.T
            re, im = (re * keep).astype(jnp.bfloat16), (im * keep).astype(jnp.bfloat16)
            out_ref[e, :, pl.ds(pl.multiple_of(tile * tall, tall), tall)] = re
            out_ref[e, :, pl.ds(pl.multiple_of(orb + tile * tall, tall), tall)] = im

    def store_diagonal():
        row, col = triangle()
        keep = kept(t)

        @pl.loop(0, nt)
        def _(e):
            packed = [
                parts[3, e, c * qr : (c + 1) * qr, h * tall : (h + 1) * tall] for c in range(nm) for h in range(2)
            ]
            both = jnp.concatenate(packed, axis=0).astype(jnp.float32)
            turned = both.T
            re = jnp.where(row > col, turned, both)
            im = jnp.where(row > col, both, jnp.where(row < col, -turned, 0.0))
            out_ref[e, :, pl.ds(pl.multiple_of(t * tall, tall), tall)] = (re * keep).astype(jnp.bfloat16)
            out_ref[e, :, pl.ds(pl.multiple_of(orb + t * tall, tall), tall)] = (im * keep).astype(jnp.bfloat16)

    forward(2)
    mix(0)
    forward(3)
    mix(1)
    mix(2)
    landed(0)
    landed(1)
    store(0, tile_at(1), False)
    store(1, tile_at(nt - 1), True)
    mix(3)
    landed(2)

    @pl.when(ring < 2)
    def _():
        store(2, tile_at(2), False)

    @pl.when(ring >= 2)
    def _():
        store(2, tile_at(2), True)

    landed(3)
    store_diagonal()

    for u in range(4):
        for kk in range(nm):
            if u < 3:
                far_copy(u, kk, part_lo(u, m)).wait_send()
            if kk > 0:
                near_copy(u, kk, m).wait_send()
        for i, j in pairs:
            if (i, j) != (0, 0):
                a_copy(u, i, j, t).wait_send()

            @pl.when(has_up)
            def _():
                z_copy(u, i, j, True).wait_send()

            @pl.when(has_down)
            def _():
                z_copy(u, i, j, False).wait_send()


def fused(green_ret, injection, mom_shift, phon_off, coupling, tile_nbr):
    nt, nm, nz = lax.axis_size("tile"), lax.axis_size("mom"), lax.axis_size("ewin")
    orbitals, width = green_ret.shape[3:]
    tall = orbitals // nt
    qr = tall // nm // 2
    green = green_ret.reshape(orbitals, width)
    gamma = injection.reshape(1, orbitals)
    vmem, smem = pl.BlockSpec(memory_space=pltpu.VMEM), pl.BlockSpec(memory_space=pltpu.SMEM)
    dma = pltpu.SemaphoreType.DMA
    total = pl.pallas_call(
        lambda *refs: fused_kernel(nt, nm, nz, *refs),
        out_shape=jax.ShapeDtypeStruct((nt, tall, width), jnp.bfloat16),
        in_specs=[vmem, vmem, smem, smem, smem, smem],
        out_specs=vmem,
        scratch_shapes=[
            pltpu.VMEM((nt, 2 * tall, width), jnp.bfloat16),
            pltpu.VMEM((nt, 2, nm, qr, 2 * tall), jnp.bfloat16),
            pltpu.VMEM((2, 2 * nm, qr, 2 * tall), jnp.bfloat16),
            pltpu.VMEM((nt, nm, qr, 2 * tall), jnp.bfloat16),
            pltpu.VMEM((3, nt, nm, 4 * qr, 2 * tall), jnp.bfloat16),
            pltpu.VMEM((nm, nt, 4 * qr, 2 * tall), jnp.bfloat16),
            pltpu.VMEM((4, nt, tall, 2 * tall), jnp.bfloat16),
            pltpu.SMEM((nm, 2 * HW + 1), jnp.float32),
            dma((4, nt, nm)),
            dma((4, nt, nm)),
            dma((2, 4, nt, nm)),
            dma((2, 4, nt, nm)),
            dma((2, 4, nm)),
            dma((2, 4, nm)),
            dma((4,)),
        ],
        compiler_params=pltpu.CompilerParams(collective_id=0, has_side_effects=True),
    )(green, gamma, mom_shift, phon_off, coupling, tile_nbr)
    return total[None, None]


def with_halo(shard, sides, width):
    for axis, dim in sides:
        peers, length = (lax.axis_size(axis), shard.shape[dim])
        up = [(i, (i + 1) % peers) for i in range(peers - 1)]
        down = [(j, i) for i, j in up]
        last = lax.slice_in_dim(shard, length - width, length, axis=dim)
        initial = lax.slice_in_dim(shard, 0, width, axis=dim)
        before = lax.ppermute(last, axis, up)
        after = lax.ppermute(initial, axis, down)
        shard = jnp.concatenate([before, shard, after], axis=dim)
    return shard


def on_device(green_ret, injection, mom_shift, phon_off, coupling, tile_nbr):
    blocks = green_ret[0, 0]
    gamma = injection[0, 0]
    orbitals = blocks.shape[1]
    ntiles = lax.axis_size("tile")
    per_tile = orbitals // ntiles
    real_part = blocks[:, :, :orbitals].astype(jnp.float32)
    imag_part = blocks[:, :, orbitals:].astype(jnp.float32)
    scale = gamma[:, None, :]
    left_re = jnp.concatenate([real_part * scale, imag_part * scale], axis=2).astype(jnp.bfloat16)
    left_im = jnp.concatenate([imag_part * scale, -real_part * scale], axis=2).astype(jnp.bfloat16)
    real_out = jnp.einsum("prk,pck->prc", left_re, blocks, preferred_element_type=jnp.float32)
    imag_out = jnp.einsum("prk,pck->prc", left_im, blocks, preferred_element_type=jnp.float32)
    payload = jnp.concatenate([real_out, imag_out], axis=2).astype(jnp.bfloat16)
    exchanged = lax.all_to_all(payload, "tile", split_axis=1, concat_axis=0, tiled=True)
    energies = exchanged.shape[0]
    rimmed = with_halo(exchanged, (("ewin", 0),), HW)
    extended = lax.all_gather(rimmed[None], "mom", axis=0, tiled=True)
    nmom = lax.axis_size("mom")
    here = lax.axis_index("mom")
    source = jnp.mod(here - mom_shift, nmom)
    onehot = (source[:, None] == jnp.arange(nmom, dtype=jnp.int32)[None, :]).astype(jnp.float32)
    weights = jnp.dot(onehot.T, coupling, precision=lax.Precision.HIGHEST)
    total = jnp.zeros(exchanged.shape, jnp.float32)
    for offset in range(NW):
        start = HW + phon_off[offset]
        piece = lax.dynamic_slice_in_dim(extended, start, energies, 1)
        for moment in range(nmom):
            total = total + weights[moment, offset] * piece[moment].astype(jnp.float32)
    tile_here = lax.axis_index("tile")
    neighbours = lax.dynamic_index_in_dim(tile_nbr, tile_here, 0, keepdims=False)
    coltile = jnp.arange(orbitals, dtype=jnp.int32) // per_tile
    colmask = jnp.any(coltile[:, None] == neighbours[None, :], axis=1).astype(jnp.float32)
    colmask = jnp.concatenate([colmask, colmask])
    result = (total * colmask[None, None, :]).astype(jnp.bfloat16)
    return result[None, None]


def body_for(mesh):
    nt, nm = mesh.shape["tile"], mesh.shape["mom"]

    def body(green_ret, *rest):
        points, orbitals = green_ret.shape[2:4]
        aligned = orbitals % (nt * LANES) == 0 and orbitals % (nt * nm * 2 * PACK) == 0
        if aligned and points == 1 and nt == HW:
            return fused(green_ret, *rest)
        return on_device(green_ret, *rest)

    return body


def solution(mesh):
    placed = (
        P("mom", "ewin", "tile", None, None),
        P("mom", "ewin", "tile", None),
        P(),
        P(),
        P(),
        P(),
    )
    return jax.shard_map(
        body_for(mesh),
        mesh=mesh,
        in_specs=placed,
        out_specs=P("mom", "ewin", None, "tile", None),
        check_vma=False,
    )
```
